256 devices in a mesh: dp: 32 (over x_lo, z, core), feat: 8 (over y, x_hi).
Axes of the slice: x: 4 (x_hi: 2, x_lo: 2; x = x_hi * 2 + x_lo), y: 4, z: 8, core: 2. Of those that a mesh axis runs over, the one named last changes fastest.
Arguments:
- proj_grads: bfloat16 [8192, 16384], P('dp', 'feat'), may hold values from -1.25 to 1.25
- val_grads: bfloat16 [16384, 128], P('feat'), may hold values from -1.25 to 1.25
Outputs:
- interactions: bfloat16 [8192, 8192], P('dp', 'feat')
- data_scores: float32 [8192, 128], P('dp')
The draws below stay inside these ranges and needn't reach their ends.
All inputs are finite; a program needn't handle non-finite values.
Results may differ from the reference program's by a relative error of at most 0.0006.
Values may be sent and summed in bfloat16 or wider, within the bound.
No kernel may reach another device: no remote copies, remote signals or barrier semaphores. Data moves between devices by JAX's collectives and lax.ppermute only.
A program may use at most 192 MiB of HBM per device.

```python
import jax
import jax.numpy as jnp
from jax import lax

K = 16384
ROWS = 256
Q = 128
EXAMPLES = 8192
N_DP = 32


def block_levels(key, shape, pieces, least, top_value):
    def one(dim, shards_of):
        heights = jax.random.uniform(jax.random.fold_in(jax.random.fold_in(key, 6), dim), (shards_of,), jnp.float32, least / len(pieces), top_value / len(pieces))
        return jnp.repeat(jnp.exp(heights), shape[dim] // shards_of).reshape((-1,) + (1,) * (len(shape) - dim - 1))

    factor_of = one(*pieces[0])
    for cut in pieces[1:]:
        factor_of = factor_of * one(*cut)
    return factor_of


def gaussian(stream_key, shape, width, bound, cuts=(), held_as=jnp.bfloat16):
    array = width * jax.random.normal(stream_key, shape, jnp.float32)
    if cuts:
        array = array * block_levels(stream_key, shape, cuts, -0.22, 0.18)
    return jnp.clip(array, -bound, bound).astype(held_as)


def setup_inputs(seed: int = 0) -> dict:
    streams_of = jax.random.split(jax.random.key(seed), 3)
    proj_grads = gaussian(streams_of[0], (EXAMPLES, K), 0.0884, 1.25, ((0, 32), (1, 8)))
    val_grads = gaussian(streams_of[1], (K, Q), 0.0884, 1.25, ((0, 8),))
    return dict(proj_grads=proj_grads, val_grads=val_grads)


def reference(proj_grads, val_grads):
    pair_weight = 1.0 / (ROWS ** 0.5)
    first = jnp.dot(proj_grads, val_grads, preferred_element_type=jnp.float32)
    blocks = proj_grads.reshape(N_DP, ROWS, K)
    bases = jnp.arange(N_DP, dtype=jnp.int32) * ROWS
    col_index = jnp.arange(ROWS * N_DP, dtype=jnp.int32)

    def one_block(inputs):
        block, base = inputs
        gram_rows = jnp.dot(block, proj_grads.T, preferred_element_type=jnp.float32)
        row_index = base + jnp.arange(ROWS, dtype=jnp.int32)
        pair_values = jnp.where(row_index[:, None] == col_index[None, :], 0.0, gram_rows)
        pair_sum = jnp.dot(pair_values, first, precision=lax.Precision.HIGHEST)
        return pair_values.astype(jnp.bfloat16), pair_sum

    inter_blocks, sum_blocks = lax.map(one_block, (blocks, bases))
    interactions = inter_blocks.reshape(ROWS * N_DP, ROWS * N_DP)
    pair_sum = sum_blocks.reshape(ROWS * N_DP, first.shape[1])
    return interactions, first - pair_weight * pair_sum
```

```python
import jax
import jax.numpy as jnp
import numpy as np
from jax import lax
from jax.sharding import PartitionSpec as P


NZ, NF = 8, 8


def row_block(a, z, k):
    return (a % 2) * 2 * NZ + (z % NZ) * 2 + (k % 2)


PLACES = [(a, z, k) for a in range(2) for z in range(NZ) for k in range(2)]


def shift(to):
    return [(row_block(*p), row_block(*to(*p))) for p in PLACES]


FROM_ABOVE = shift(lambda a, z, k: (a, z - 1, k))
FROM_BELOW = shift(lambda a, z, k: (a, z + 1, k))
OTHER_COLUMN = shift(lambda a, z, k: (1 - a, z, k))
OTHER_CORE = shift(lambda a, z, k: (a, z, 1 - k))


def pair_lists(a, z, k):
    o, j = 1 - a, 1 - k
    sel = k if a == 0 else j
    far = k if z < NZ // 2 else j
    blk = row_block
    one = [
        (blk(a, z - 1, k), blk(a, z + 1, k)),
        (blk(a, z - 1, k), blk(a, z + 1, j)),
        (blk(a, z - 1, k), blk(o, z, k)),
        (blk(a, z - 1, k), blk(o, z, j)),
        (blk(a, z, k), blk(a, z + 1, k)),
        (blk(a, z, k), blk(a, z + 1, j)),
        (blk(a, z, k), blk(a, z, j)),
        (blk(a, z, k), blk(o, z, sel)),
    ]
    two = [
        (blk(a, z - 2, k), blk(a, z + 1, k)),
        (blk(a, z - 2, k), blk(a, z + 1, j)),
        (blk(a, z - 2, k), blk(a, z + 2, far)),
        (blk(a, z - 2, k), blk(o, z, k)),
        (blk(a, z - 2, k), blk(o, z, j)),
        (blk(a, z - 1, k), blk(o, z + 2, k)),
        (blk(a, z - 1, k), blk(o, z + 2, j)),
        (blk(a, z - 2, k), blk(o, z + 2, sel)),
    ]
    return one, two


def colour_edges(edges, n_colours):
    at_src, at_dst = {}, {}
    colour = [None] * len(edges)

    def free(table, node):
        return next(c for c in range(n_colours) if (node, c) not in table)

    for e, (s, d) in enumerate(edges):
        c1, c2 = free(at_src, s), free(at_dst, d)
        if c1 != c2:
            path, node, side, c = [], d, 1, c1
            while True:
                nxt = (at_dst if side else at_src).get((node, c))
                if nxt is None:
                    break
                path.append(nxt)
                node = edges[nxt][0 if side else 1]
                side, c = 1 - side, c1 + c2 - c
            for q in path:
                at_src.pop((edges[q][0], colour[q]))
                at_dst.pop((edges[q][1], colour[q]))
            for q in path:
                colour[q] = c1 + c2 - colour[q]
                at_src[(edges[q][0], colour[q])] = q
                at_dst[(edges[q][1], colour[q])] = q
        colour[e] = c1
        at_src[(s, c1)] = e
        at_dst[(d, c1)] = e
    return colour


def routes():
    per = len(PLACES) // NF
    edges, what = [], []
    for p in PLACES:
        for round_, pairs in enumerate(pair_lists(*p)):
            for f, (r, c) in enumerate(pairs):
                src = row_block(*p) * NF + f
                edges.append((src, r * NF + c // per))
                what.append((2 * round_, c % per))
                if not (round_ == 0 and f == 6):
                    edges.append((src, c * NF + r // per))
                    what.append((2 * round_ + 1, r % per))
    colour = colour_edges(edges, 4)
    n = len(PLACES) * NF
    perms = [[] for _ in range(4)]
    sends = np.zeros((n, 4), np.int32)
    takes = np.full((n, 4), -1, np.int32)
    for (s, d), (item, at), c in zip(edges, what, colour):
        perms[c].append((s, d))
        sends[s, c] = item
        assert takes[d, at] < 0
        takes[d, at] = c
    for i in range(len(PLACES)):
        assert takes[i * NF + i // per, i % per] < 0
        takes[i * NF + i // per, i % per] = 4
    assert (takes >= 0).all()
    return perms, sends, takes


def exchange(value, axis):
    return lax.all_to_all(value, axis, split_axis=0, concat_axis=0, tiled=True)


def sum_over(value, axis):
    n = lax.axis_size(axis)
    return exchange(jnp.broadcast_to(value, (n, *value.shape)), axis).sum(axis=0)


def pair_tile(left_rows, right_rows):
    return lax.dot_general(
        left_rows, right_rows, (((1,), (1,)), ((), ())), preferred_element_type=jnp.float32
    )


def parts_of(x):
    high = lax.reduce_precision(x, 8, 7)
    rest = x - high
    mid = lax.reduce_precision(rest, 8, 7)
    return jnp.concatenate([high, mid, rest - mid], axis=-1).astype(jnp.bfloat16)


def three(y):
    q = y.shape[-1] // 3
    return (y[:, 2 * q :] + y[:, q : 2 * q]) + y[:, :q]


def body(proj_grads, val_grads):
    rows = proj_grads.shape[0]
    pair_weight = 1.0 / rows**0.5
    perms, sends, takes = routes()
    dp = lax.axis_index("dp")
    feat = lax.axis_index("feat")
    me = dp * NF + feat
    column_0 = dp < 2 * NZ
    low_half = (dp // 2) % NZ < NZ // 2

    def dp_move(x, perm):
        return lax.ppermute(x, "dp", perm)

    own = proj_grads
    up1 = dp_move(own, FROM_ABOVE)
    down1 = dp_move(own, FROM_BELOW)
    side = dp_move(own, OTHER_COLUMN)
    own_ = dp_move(own, OTHER_CORE)

    first = sum_over(
        jnp.dot(own, val_grads, preferred_element_type=jnp.float32), "feat"
    )
    norms = jnp.sum(jnp.square(own.astype(jnp.float32)), axis=1, keepdims=True)
    back = three(
        lax.dot_general(
            own, parts_of(first), (((0,), (0,)), ((), ())), preferred_element_type=jnp.float32
        )
    )
    n_dp = lax.axis_size("dp")
    back = exchange(back.reshape(n_dp, -1, back.shape[1]), "dp").sum(axis=0)
    back = exchange(jnp.broadcast_to(back, (n_dp, *back.shape)), "dp")
    back = back.reshape(-1, back.shape[-1])
    partial_sum = three(jnp.dot(own, parts_of(back), preferred_element_type=jnp.float32))
    pair_sum = sum_over(partial_sum - norms * first, "feat")
    data_scores = first - pair_weight * pair_sum

    eye = jnp.arange(rows)[:, None] == jnp.arange(rows)[None, :]
    diagonal = jnp.where(eye, 0.0, pair_tile(own, own))
    diagonal = exchange(diagonal.reshape(NF, rows // NF, rows), "feat").sum(axis=0)
    diagonal = diagonal.astype(jnp.bfloat16)
    diagonal = exchange(jnp.broadcast_to(diagonal, (NF, *diagonal.shape)), "feat")
    diagonal = diagonal.reshape(rows, rows)

    up1_ = dp_move(up1, OTHER_CORE)
    side_ = dp_move(side, OTHER_CORE)
    one = [
        pair_tile(down1, up1),
        pair_tile(down1, up1_),
        pair_tile(down1, side),
        pair_tile(down1, side_),
        pair_tile(own, up1),
        pair_tile(own, up1_),
        pair_tile(own, own_),
        pair_tile(own, jnp.where(column_0, side, side_)),
    ]
    one = exchange(jnp.stack(one), "feat").sum(axis=0)

    up2 = dp_move(up1, FROM_ABOVE)
    down2 = dp_move(down1, FROM_BELOW)
    up2_ = dp_move(up2, OTHER_CORE)
    far = dp_move(up2, OTHER_COLUMN)
    far_ = dp_move(far, OTHER_CORE)
    two = [
        pair_tile(down2, up1),
        pair_tile(down2, up1_),
        pair_tile(down2, jnp.where(low_half, up2, up2_)),
        pair_tile(down2, side),
        pair_tile(down2, side_),
        pair_tile(down1, far),
        pair_tile(down1, far_),
        pair_tile(down2, jnp.where(column_0, far, far_)),
    ]
    two = exchange(jnp.stack(two), "feat").sum(axis=0)

    one, two = one.astype(jnp.bfloat16), two.astype(jnp.bfloat16)
    items = jnp.stack([one, one.T, two, two.T])
    send = jnp.asarray(sends)[me]
    got = [
        lax.ppermute(
            lax.dynamic_index_in_dim(items, send[c], 0, keepdims=False), ("dp", "feat"), perms[c]
        )
        for c in range(4)
    ]
    got = jnp.stack([*got, diagonal])
    take = jnp.asarray(takes)[me]
    interactions = jnp.concatenate(
        [lax.dynamic_index_in_dim(got, take[s], 0, keepdims=False) for s in range(4)], axis=1
    )
    return interactions, data_scores


def solution(mesh):
    return jax.shard_map(
        body,
        mesh=mesh,
        in_specs=(P("dp", "feat"), P("feat", None)),
        out_specs=(P("dp", "feat"), P("dp", None)),
        check_vma=False,
    )
```

```python
import functools

import jax
import jax.numpy as jnp
import numpy as np
from jax import lax
from jax.experimental import pallas as pl
from jax.experimental.pallas import tpu as pltpu
from jax.sharding import PartitionSpec as P


NZ, NF = 8, 8


def row_block(a, z, k):
    return (a % 2) * 2 * NZ + (z % NZ) * 2 + (k % 2)


PLACES = [(a, z, k) for a in range(2) for z in range(NZ) for k in range(2)]


def shift(to):
    return [(row_block(*p), row_block(*to(*p))) for p in PLACES]


FROM_ABOVE = shift(lambda a, z, k: (a, z - 1, k))
FROM_BELOW = shift(lambda a, z, k: (a, z + 1, k))
OTHER_COLUMN = shift(lambda a, z, k: (1 - a, z, k))
OTHER_CORE = shift(lambda a, z, k: (a, z, 1 - k))


CHIP_GROUPS = [[row_block(a, z, k) for a in range(2) for z in range(NZ)] for k in range(2)]


def pair_lists(a, z, k):
    o, j = 1 - a, 1 - k
    sel = k if a == 0 else j
    low = k if z < NZ // 2 else j
    blk = row_block
    one = [
        (blk(a, z - 1, k), blk(a, z + 1, k)),
        (blk(a, z - 1, j), blk(a, z + 1, k)),
        (blk(a, z - 1, k), blk(o, z, k)),
        (blk(a, z - 1, j), blk(o, z, k)),
        (blk(a, z, k), blk(a, z + 1, k)),
        (blk(a, z, j), blk(a, z + 1, k)),
        (blk(a, z, j), blk(a, z, k)),
        (blk(a, z, sel), blk(o, z, k)),
    ]
    two = [
        (blk(a, z - 2, k), blk(a, z + 1, k)),
        (blk(a, z - 2, j), blk(a, z + 1, k)),
        (blk(a, z - 2, k), blk(o, z, k)),
        (blk(a, z - 2, j), blk(o, z, k)),
        (blk(a, z - 2, low), blk(a, z + 2, k)),
        (blk(a, z - 1, k), blk(o, z + 2, k)),
        (blk(a, z - 1, j), blk(o, z + 2, k)),
        (blk(a, z - 2, sel), blk(o, z + 2, k)),
    ]
    return one, two


def colour_edges(edges, n_colours):
    at_src, at_dst = {}, {}
    colour = [None] * len(edges)

    def free(table, node):
        return next(c for c in range(n_colours) if (node, c) not in table)

    for e, (s, d) in enumerate(edges):
        c1, c2 = free(at_src, s), free(at_dst, d)
        if c1 != c2:
            path, node, side, c = [], d, 1, c1
            while True:
                nxt = (at_dst if side else at_src).get((node, c))
                if nxt is None:
                    break
                path.append(nxt)
                node = edges[nxt][0 if side else 1]
                side, c = 1 - side, c1 + c2 - c
            for q in path:
                at_src.pop((edges[q][0], colour[q]))
                at_dst.pop((edges[q][1], colour[q]))
            for q in path:
                colour[q] = c1 + c2 - colour[q]
                at_src[(edges[q][0], colour[q])] = q
                at_dst[(edges[q][1], colour[q])] = q
        colour[e] = c1
        at_src[(s, c1)] = e
        at_dst[(d, c1)] = e
    return colour


def hops(a, z, f, i, g):
    steps = ((f % 2 * 2 + a - g % 2 * 2 - i // (2 * NZ), 4), (f // 2 - g // 2, 4), (z - i // 2, NZ))
    return sum(min(d % n, -d % n) for d, n in steps)


def reducers():
    per = len(PLACES) // NF
    table = np.zeros((len(PLACES), 2, NF), np.int32)
    for a, z, k in PLACES:
        for round_, pairs in enumerate(pair_lists(a, z, k)):
            cost = [
                [
                    hops(a, z, f, r, c // per) ** 3 + hops(a, z, f, c, r // per) ** 3
                    for f in range(NF)
                ]
                for r, c in pairs
            ]
            at, better = list(range(NF)), True
            while better:
                better = False
                for p in range(NF):
                    for q in range(p):
                        now = cost[p][at[p]] + cost[q][at[q]]
                        if cost[p][at[q]] + cost[q][at[p]] < now:
                            at[p], at[q], better = at[q], at[p], True
            table[row_block(a, z, k), round_] = at
    return table


def routes(table):
    per = len(PLACES) // NF
    edges, what = [], []
    for p in PLACES:
        for round_, pairs in enumerate(pair_lists(*p)):
            for slot, (r, c) in enumerate(pairs):
                src = row_block(*p) * NF + int(table[row_block(*p), round_, slot])
                edges.append((src, r * NF + c // per))
                what.append((2 * round_, c % per))
                if not (round_ == 0 and slot == 6):
                    edges.append((src, c * NF + r // per))
                    what.append((2 * round_ + 1, r % per))
    colour = colour_edges(edges, 4)
    n = len(PLACES) * NF
    perms = [[] for _ in range(4)]
    sends = np.zeros((n, 4), np.int32)
    takes = np.full((n, 4), -1, np.int32)
    for (s, d), (item, at), c in zip(edges, what, colour):
        perms[c].append((s, d))
        sends[s, c] = item
        assert takes[d, at] < 0
        takes[d, at] = c
    for i in range(len(PLACES)):
        assert takes[i * NF + i // per, i % per] < 0
        takes[i * NF + i // per, i % per] = 4
    assert (takes >= 0).all()
    return perms, sends, takes


def exchange(value, axis, groups=None):
    return lax.all_to_all(
        value, axis, split_axis=0, concat_axis=0, tiled=True, axis_index_groups=groups
    )


def parts_of(x):
    high = x.astype(jnp.bfloat16)
    rest = x - high.astype(jnp.float32)
    mid = rest.astype(jnp.bfloat16)
    low = (rest - mid.astype(jnp.float32)).astype(jnp.bfloat16)
    return jnp.concatenate([high, mid, low], axis=-1)


def three(y):
    q = y.shape[-1] // 3
    return (y[:, 2 * q :] + y[:, q : 2 * q]) + y[:, :q]


def hdot_kernel(core, own, part, part_, first, mine, other):
    value = part[...] + part_[...]
    first[...] = value
    terms = parts_of(value)
    half = mine.shape[0]
    for at in range(2):
        rows = three(
            lax.dot_general(
                own[:, at * half : (at + 1) * half],
                terms,
                (((0,), (0,)), ((), ())),
                preferred_element_type=jnp.float32,
            )
        )

        @pl.when(core[0] == at)
        def _():
            mine[...] = rows

        @pl.when(core[0] != at)
        def _():
            other[...] = rows


def gdot_kernel(core, own, mine, other, first, one, one_, out):
    half = mine.shape[0]
    total = None
    for at in range(2):
        back = jnp.where(core[0] == at, mine[...], other[...])
        term = three(
            jnp.dot(
                own[:, at * half : (at + 1) * half], parts_of(back), preferred_element_type=jnp.float32
            )
        )
        total = term if total is None else total + term
    wide = own[...].astype(jnp.float32)
    rows, q = first.shape
    out[:rows] = total - jnp.sum(wide * wide, axis=1, keepdims=True) * first[...]
    square = one[2 * rows :] + one_[rows:]
    piece = square.shape[0]
    out[rows : rows + piece] = square[:, :q]
    out[rows + piece :] = square[:, q:]


def tile(left, right):
    return lax.dot_general(
        left, right, (((1,), (1,)), ((), ())), preferred_element_type=jnp.float32
    )


def products(plan, ins, flags):
    for left, right in plan:
        if isinstance(left, tuple):
            i, j, flag = left
            value = jnp.where(flags[flag] > 0, ins[i][...], ins[j][...])
        else:
            value = ins[left][...]
        if isinstance(right, tuple):
            against = jnp.concatenate([ins[i][...] for i in right], axis=0)
        else:
            against = ins[right][...]
        yield tile(value, against)


UP = (4, 5)
PLAN_1 = ((0, UP), (1, UP), (2, UP), (3, UP), (0, 6), (1, 6), ((2, 3, 0), 6), (3, 2))
SLOTS_1 = (0, 1, 4, 5, 2, 3, 7, 6)
PLAN_2A = ((0, (2, 3)), (1, (2, 3)), (0, 4), (1, 4))
PLAN_2B = (((0, 1, 1), (4, 5)), (2, (6, 7)), (3, (6, 7)), ((0, 1, 0), (6, 7)))


def kernel_1(flags, order, y, *refs):
    ins, outs, acc = refs[:7], refs[7:11], refs[11]
    for slot, product in zip(SLOTS_1, products(PLAN_1, ins, flags)):
        acc[order[0, slot]] = product
    square = tile(ins[2][...], ins[2][...])
    rows = square.shape[0]
    own = lax.broadcasted_iota(jnp.int32, (rows, rows), 0)
    other = lax.broadcasted_iota(jnp.int32, (rows, rows), 1)
    acc[NF] = jnp.where(own == other, 0.0, square)
    piece = 2 * rows // NF
    for dy, out in enumerate(outs):
        out[:rows] = acc[2 * dy]
        out[rows : 2 * rows] = acc[2 * dy + 1]
        at = pl.multiple_of((y[0] ^ dy) * piece, piece)
        out[2 * rows :] = acc[NF, pl.ds(at, piece)]


def kernel_2a(flags, *refs):
    for slot, product in enumerate(products(PLAN_2A, refs[:5], flags)):
        refs[5][slot] = product


def kernel_2b(flags, order, *refs):
    ins, early, along_y, along_x, acc = refs[:8], refs[8], refs[9:13], refs[13:15], refs[15]
    for slot, product in enumerate(products(PLAN_2B, ins, flags)):
        acc[order[1, NF // 2 + slot]] = product
    for slot in range(NF // 2):
        acc[order[1, slot]] = early[slot]
    cut = along_y[0].shape[1]
    for s in range(NF):
        along_y[s // 2][s % 2] = acc[s, :cut]
        along_x[s % 2][s // 2] = acc[s, cut:]


def mid_kernel(a, b, c, d, low, low_, keep, send, *lowers):
    upper = (a[...] + b[...]) + (c[...] + d[...])
    keep[...] = upper[0]
    send[...] = upper[1]
    for dy, out in enumerate(lowers):
        out[...] = low[dy] + low_[dy]


def items_kernel(sends, one_ref, one_ref_, up, up_, a, b, c, d, *outs):
    rows = one_ref.shape[1]
    one = one_ref[:rows] + one_ref_[:rows]
    lower = (a[...] + b[...]) + (c[...] + d[...])
    two = jnp.concatenate([up[...] + up_[...], lower], axis=0)
    choices = [x.astype(jnp.bfloat16) for x in (one, one.T, two, two.T)]
    for n, out in enumerate(outs):
        value = choices[3]
        for q in (2, 1, 0):
            value = jnp.where(sends[n] == q, choices[q], value)
        out[...] = value


def place_kernel(weight, takes, y, *refs):
    got, pieces, (total, total_, first), (out, scores), diagonal = (
        refs[:4], refs[4:8], refs[8:11], refs[11:13], refs[13]
    )
    rows = out.shape[0]
    piece = 2 * rows // NF
    half = first.shape[1]
    for dy, source in enumerate(pieces):
        at = pl.multiple_of((y[0] ^ dy) * piece, piece)
        diagonal[pl.ds(at, piece), :half] = source[rows : rows + piece].astype(jnp.bfloat16)
        diagonal[pl.ds(at, piece), half:] = source[rows + piece :].astype(jnp.bfloat16)
    values = [x[...] for x in got]
    for s in range(4):
        value = diagonal[...]
        for q in range(4):
            value = jnp.where(takes[s] == q, values[q], value)
        out[:, s * rows : (s + 1) * rows] = value
    scores[...] = first[...] - weight * (total[...] + total_[...])


def call(kernel, scalars, operands, outs, scratch=(), flops=0):
    vmem = pl.BlockSpec(memory_space=pltpu.VMEM)
    moved = sum(x.size * x.dtype.itemsize for x in (*operands, *outs))
    return pl.pallas_call(
        kernel,
        in_specs=[pl.BlockSpec(memory_space=pltpu.SMEM)] * len(scalars) + [vmem] * len(operands),
        out_specs=[vmem] * len(outs),
        out_shape=list(outs),
        scratch_shapes=list(scratch),
        compiler_params=pltpu.CompilerParams(vmem_limit_bytes=24 * 2**20),
        cost_estimate=pl.CostEstimate(flops=flops, bytes_accessed=moved, transcendentals=0),
    )(*scalars, *operands)


def array(dtype, *shape):
    return jax.ShapeDtypeStruct(shape, dtype)


def body(proj_grads, val_grads):
    rows, depth = proj_grads.shape
    pair_weight = 1.0 / rows**0.5
    tile_flops = 2 * rows * rows * depth
    table = reducers()
    perms, sends, takes = routes(table)
    dp = lax.axis_index("dp")
    feat = lax.axis_index("feat")
    me = dp * NF + feat
    column_0 = dp < 2 * NZ
    low_half = (dp // 2) % NZ < NZ // 2
    core = dp % 2
    flags = jnp.stack([column_0, low_half]).astype(jnp.int32)
    order = jnp.asarray(table)[dp] ^ feat
    y = feat // 2
    send = jnp.asarray(sends)[me]
    take = jnp.asarray(takes)[me]
    f32, bf16 = jnp.float32, jnp.bfloat16

    def move(x, perm):
        return lax.ppermute(x, "dp", perm)

    def from_feat(x, s):
        return lax.ppermute(x, "feat", [(f, f ^ s) for f in range(NF)])

    def over_y(parts, n=None):
        parts = [parts[0]] + [from_feat(parts[dy], 2 * dy) for dy in (1, 2, 3)]
        a, b, c, d = [p[:n] for p in parts]
        return (a + b) + (c + d), parts

    own = proj_grads
    cut = rows // 2
    up1 = [move(own[:cut], FROM_ABOVE), move(own[cut:], FROM_ABOVE)]
    down1 = move(own, FROM_BELOW)
    side = move(own, OTHER_COLUMN)
    own_ = move(own, OTHER_CORE)

    first = jnp.dot(own, val_grads, preferred_element_type=f32)
    first, _ = over_y([first] * 4)
    first_ = from_feat(first, 1)

    high = 3 * rows // 4
    up2 = [move(up1[0], FROM_ABOVE), move(up1[1], FROM_ABOVE)]
    down2 = move(down1, FROM_BELOW)
    down1_ = move(down1, OTHER_CORE)

    one = call(
        kernel_1,
        (flags, order, y[None]),
        (down1, down1_, own, own_, *up1, side),
        [array(f32, 2 * rows + 2 * rows // NF, rows)] * 4,
        [pltpu.VMEM((NF + 1, rows, rows), f32)],
        (NF + 1) * tile_flops,
    )
    one, _ = over_y(one)

    half = depth // 2
    q = first.shape[1]
    first, mine, other = call(
        hdot_kernel,
        (core[None],),
        (own, first, first_),
        [array(f32, rows, q), array(f32, half, q), array(f32, half, q)],
        flops=6 * rows * depth * q,
    )
    mine = mine + move(other, OTHER_CORE)
    chips = 2 * NZ
    mine = exchange(mine.reshape(chips, -1, mine.shape[1]), "dp", CHIP_GROUPS)
    mine = mine.sum(axis=0)
    mine = exchange(jnp.broadcast_to(mine, (chips, *mine.shape)), "dp", CHIP_GROUPS)
    mine = mine.reshape(half, -1)

    far = [move(up2[0], OTHER_COLUMN), move(up2[1], OTHER_COLUMN)]
    down2_ = move(down2, OTHER_CORE)
    (early,) = call(
        kernel_2a,
        (flags,),
        (down2, down2_, *up1, side),
        [array(f32, NF // 2, rows, rows)],
        flops=4 * tile_flops,
    )
    two = call(
        kernel_2b,
        (flags, order),
        (down2, down2_, down1, down1_, *up2, *far, early),
        [array(f32, 2, high, rows)] * 4 + [array(f32, 4, rows - high, rows)] * 2,
        [pltpu.VMEM((NF, rows, rows), f32)],
        4 * tile_flops,
    )
    upper = [two[0]] + [from_feat(two[dy], 2 * dy) for dy in (1, 2, 3)]
    lower_ = from_feat(two[5], 1)
    one_ = from_feat(one[rows:], 1)
    piece = 2 * rows // NF
    upper, send_, *lower = call(
        mid_kernel,
        (),
        (*upper, two[4], lower_),
        [array(f32, high, rows)] * 2 + [array(f32, rows - high, rows)] * 4,
    )
    upper_ = from_feat(send_, 1)
    lower = [lower[0]] + [from_feat(lower[dy], 2 * dy) for dy in (1, 2, 3)]

    other = move(mine, OTHER_CORE)
    (shared,) = call(
        gdot_kernel,
        (core[None],),
        (own, mine, other, first, one, one_),
        [array(f32, rows + 2 * piece, q)],
        flops=6 * rows * depth * q,
    )
    total, pieces = over_y([shared] * 4, rows)
    total_ = from_feat(total, 1)

    out = call(items_kernel, (send,), (one, one_, upper, upper_, *lower), [array(bf16, rows, rows)] * 4)
    got = []
    for c in range(4):
        got.append(lax.ppermute(out[c], ("dp", "feat"), perms[c]))
    return tuple(
        call(
            functools.partial(place_kernel, pair_weight),
            (take, y[None]),
            (*got, *pieces, total, total_, first),
            [array(bf16, rows, 4 * rows), array(f32, rows, q)],
            [pltpu.VMEM((rows, rows), bf16)],
        )
    )


def solution(mesh):
    return jax.shard_map(
        body,
        mesh=mesh,
        in_specs=(P("dp", "feat"), P("feat", None)),
        out_specs=(P("dp", "feat"), P("dp", None)),
        check_vma=False,
    )
```

```python
import functools

import jax
import jax.numpy as jnp
import numpy as np
from jax import lax
from jax.experimental import pallas as pl
from jax.experimental.pallas import tpu as pltpu
from jax.sharding import PartitionSpec as P


NZ, NF = 8, 8


def row_block(a, z, k):
    return (a % 2) * 2 * NZ + (z % NZ) * 2 + (k % 2)


PLACES = [(a, z, k) for a in range(2) for z in range(NZ) for k in range(2)]


def shift(to):
    return [(row_block(*p), row_block(*to(*p))) for p in PLACES]


FROM_ABOVE = shift(lambda a, z, k: (a, z - 1, k))
FROM_BELOW = shift(lambda a, z, k: (a, z + 1, k))
OTHER_COLUMN = shift(lambda a, z, k: (1 - a, z, k))
OTHER_CORE = shift(lambda a, z, k: (a, z, 1 - k))


CHIP_GROUPS = [[row_block(a, z, k) for a in range(2) for z in range(NZ)] for k in range(2)]


def pair_lists(a, z, k):
    o, j = 1 - a, 1 - k
    sel = k if a == 0 else j
    low = k if z < NZ // 2 else j
    blk = row_block
    one = [
        (blk(a, z - 1, k), blk(a, z + 1, k)),
        (blk(a, z - 1, j), blk(a, z + 1, k)),
        (blk(a, z - 1, k), blk(o, z, k)),
        (blk(a, z - 1, j), blk(o, z, k)),
        (blk(a, z, k), blk(a, z + 1, k)),
        (blk(a, z, j), blk(a, z + 1, k)),
        (blk(a, z, j), blk(a, z, k)),
        (blk(a, z, sel), blk(o, z, k)),
    ]
    two = [
        (blk(a, z - 2, k), blk(a, z + 1, k)),
        (blk(a, z - 2, j), blk(a, z + 1, k)),
        (blk(a, z - 2, k), blk(o, z, k)),
        (blk(a, z - 2, j), blk(o, z, k)),
        (blk(a, z - 2, low), blk(a, z + 2, k)),
        (blk(a, z - 1, k), blk(o, z + 2, k)),
        (blk(a, z - 1, j), blk(o, z + 2, k)),
        (blk(a, z - 2, sel), blk(o, z + 2, k)),
    ]
    return one, two


def colour_edges(edges, n_colours):
    at_src, at_dst = {}, {}
    colour = [None] * len(edges)

    def free(table, node):
        return next(c for c in range(n_colours) if (node, c) not in table)

    for e, (s, d) in enumerate(edges):
        c1, c2 = free(at_src, s), free(at_dst, d)
        if c1 != c2:
            path, node, side, c = [], d, 1, c1
            while True:
                nxt = (at_dst if side else at_src).get((node, c))
                if nxt is None:
                    break
                path.append(nxt)
                node = edges[nxt][0 if side else 1]
                side, c = 1 - side, c1 + c2 - c
            for q in path:
                at_src.pop((edges[q][0], colour[q]))
                at_dst.pop((edges[q][1], colour[q]))
            for q in path:
                colour[q] = c1 + c2 - colour[q]
                at_src[(edges[q][0], colour[q])] = q
                at_dst[(edges[q][1], colour[q])] = q
        colour[e] = c1
        at_src[(s, c1)] = e
        at_dst[(d, c1)] = e
    return colour


SIZES = (2 * 2, NF // 2, NZ)


def chip(i, f):
    return f % 2 * 2 + i // (2 * NZ), f // 2, i // 2 % NZ


def links(src, dst, memo):
    if (src, dst) not in memo:
        at, part = [], []
        for k, axes in enumerate(((2, 1, 0), (2, 0, 1))):
            here = list(src)
            for axis in axes:
                n = SIZES[axis]
                ahead = (dst[axis] - here[axis]) % n
                ways = [(1, ahead), (-1, n - ahead)]
                short = [w for w in ways if w[1] == min(ahead, n - ahead)]
                for sign, steps in short:
                    now = list(here)
                    for _ in range(steps):
                        at.append(np.ravel_multi_index((k, axis, (1 + sign) // 2, *now), (2, 3, 2, *SIZES)))
                        part.append(1.0 / len(short))
                        now[axis] = (now[axis] + sign) % n
                here[axis] = dst[axis]
        memo[src, dst] = np.array(at, np.int64), np.array(part)
    return memo[src, dst]


def reducers():
    per = len(PLACES) // NF
    table = np.tile(np.arange(NF, dtype=np.int32), (len(PLACES), 2, 1))
    memo, load, owners, far = {}, np.zeros(2 * 3 * 2 * len(PLACES) * NF // 2), {}, {}
    for p in PLACES:
        i = row_block(*p)
        for round_, pairs in enumerate(pair_lists(*p)):
            for slot, (r, c) in enumerate(pairs):
                ends = [chip(r, c // per), chip(c, r // per)][: 1 if (round_, slot) == (0, 6) else 2]
                owners[i, round_, slot] = ends
                for f in range(NF):
                    hops = [
                        sum(min((x - y) % n, (y - x) % n) for x, y, n in zip(chip(i, f), dst, SIZES))
                        for dst in ends
                    ]
                    far[i, round_, slot, f] = 30 * sum(h**3 for h in hops)

    def put(key, f, weight):
        for dst in owners[key]:
            at, part = links(chip(key[0], f), dst, memo)
            np.add.at(load, at, weight * part)

    def swap(a, b, f, g):
        for key, old, new in ((a, f, g), (b, g, f)):
            put(key, old, -1)
            put(key, new, 1)

    for key in owners:
        put(key, int(table[key]), 1)
    for sweep in range(10):
        power = 4 if sweep >= 3 else 0
        for i in range(len(PLACES)):
            for round_ in range(2):
                for p in range(NF):
                    for q in range(p):
                        a, b = (i, round_, p), (i, round_, q)
                        f, g = int(table[a]), int(table[b])
                        before = (load**power).sum() + far[(*a, f)] + far[(*b, g)]
                        swap(a, b, f, g)
                        if (load**power).sum() + far[(*a, g)] + far[(*b, f)] < before - 1e-6:
                            table[a], table[b] = g, f
                        else:
                            swap(a, b, g, f)
    return table


def routes(table):
    per = len(PLACES) // NF
    edges, what = [], []
    for p in PLACES:
        for round_, pairs in enumerate(pair_lists(*p)):
            for slot, (r, c) in enumerate(pairs):
                src = row_block(*p) * NF + int(table[row_block(*p), round_, slot])
                edges.append((src, r * NF + c // per))
                what.append((2 * round_, c % per))
                if not (round_ == 0 and slot == 6):
                    edges.append((src, c * NF + r // per))
                    what.append((2 * round_ + 1, r % per))
    colour = colour_edges(edges, 4)
    n = len(PLACES) * NF
    perms = [[] for _ in range(4)]
    sends = np.zeros((n, 4), np.int32)
    takes = np.full((n, 4), -1, np.int32)
    for (s, d), (item, at), c in zip(edges, what, colour):
        perms[c].append((s, d))
        sends[s, c] = item
        assert takes[d, at] < 0
        takes[d, at] = c
    for i in range(len(PLACES)):
        assert takes[i * NF + i // per, i % per] < 0
        takes[i * NF + i // per, i % per] = 4
    assert (takes >= 0).all()
    return perms, sends, takes


COLUMN_0, LOW_HALF, CORE, Y, AT, SENDS, TAKES = 0, 1, 2, 3, 4, 4 + 2 * NF, 8 + 2 * NF


def facts(table, sends, takes):
    rows = np.zeros((len(PLACES) * NF, 12 + 2 * NF), np.int32)
    for a, z, k in PLACES:
        i = row_block(a, z, k)
        for f in range(NF):
            at = table[i] ^ f
            rows[i * NF + f] = [
                a == 0, z < NZ // 2, k, f // 2, *at[0], *at[1], *sends[i * NF + f], *takes[i * NF + f]
            ]
    return rows


def exchange(value, axis, groups=None):
    return lax.all_to_all(
        value, axis, split_axis=0, concat_axis=0, tiled=True, axis_index_groups=groups
    )


def parts_of(x):
    high = x.astype(jnp.bfloat16)
    rest = x - high.astype(jnp.float32)
    mid = rest.astype(jnp.bfloat16)
    low = (rest - mid.astype(jnp.float32)).astype(jnp.bfloat16)
    return jnp.concatenate([high, mid, low], axis=-1)


def three(y):
    q = y.shape[-1] // 3
    return (y[:, 2 * q :] + y[:, q : 2 * q]) + y[:, :q]


def hdot_kernel(info, own, part, part_, first, mine, other):
    value = part[...] + part_[...]
    first[...] = value
    terms = parts_of(value)
    half = mine.shape[0]
    for at in range(2):
        rows = three(
            lax.dot_general(
                own[:, at * half : (at + 1) * half],
                terms,
                (((0,), (0,)), ((), ())),
                preferred_element_type=jnp.float32,
            )
        )

        @pl.when(info[CORE] == at)
        def _():
            mine[...] = rows

        @pl.when(info[CORE] != at)
        def _():
            other[...] = rows


def gdot_kernel(info, own, mine, other, first, one, one_, out):
    half = mine.shape[0]
    total = None
    for at in range(2):
        back = jnp.where(info[CORE] == at, mine[...], other[...])
        term = three(
            jnp.dot(
                own[:, at * half : (at + 1) * half], parts_of(back), preferred_element_type=jnp.float32
            )
        )
        total = term if total is None else total + term
    wide = own[...].astype(jnp.float32)
    rows, q = first.shape
    out[:rows] = total - jnp.sum(wide * wide, axis=1, keepdims=True) * first[...]
    square = one[rows:] + one_[rows:]
    piece = square.shape[0]
    out[rows : rows + piece] = square[:, :q]
    out[rows + piece :] = square[:, q:]


def tile(left, right):
    return lax.dot_general(
        left, right, (((1,), (1,)), ((), ())), preferred_element_type=jnp.float32
    )


def products(plan, ins, info):
    for left, right in plan:
        if isinstance(left, tuple):
            i, j, flag = left
            value = jnp.where(info[flag] > 0, ins[i][...], ins[j][...])
        else:
            value = ins[left][...]
        if isinstance(right, tuple):
            against = jnp.concatenate([ins[i][...] for i in right], axis=0)
        else:
            against = ins[right][...]
        yield tile(value, against)


UP = (4, 5)
PLAN_1 = ((0, UP), (1, UP), (2, UP), (3, UP), (0, 6), (1, 6), ((2, 3, COLUMN_0), 6), (3, 2))
SLOTS_1 = (0, 1, 4, 5, 2, 3, 7, 6)
PLAN_2A = ((0, (2, 3)), (1, (2, 3)), (0, 4), (1, 4))
PLAN_2B = (((0, 1, LOW_HALF), (4, 5)), (2, (6, 7)), (3, (6, 7)), ((0, 1, COLUMN_0), (6, 7)))


def kernel_1(info, *refs):
    ins, outs, acc = refs[:7], refs[7:11], refs[11]
    for slot, product in zip(SLOTS_1, products(PLAN_1, ins, info)):
        acc[info[AT + slot]] = product
    square = tile(ins[2][...], ins[2][...])
    rows = square.shape[0]
    own = lax.broadcasted_iota(jnp.int32, (rows, rows), 0)
    other = lax.broadcasted_iota(jnp.int32, (rows, rows), 1)
    acc[NF] = jnp.where(own == other, 0.0, square)
    piece = 2 * rows // NF
    for dy, out in enumerate(outs):
        out[:rows] = acc[2 * dy]
        out[rows : 2 * rows] = acc[2 * dy + 1]
        at = pl.multiple_of((info[Y] ^ dy) * piece, piece)
        out[2 * rows :] = acc[NF, pl.ds(at, piece)]


def kernel_2a(info, *refs):
    for slot, product in enumerate(products(PLAN_2A, refs[:5], info)):
        refs[5][slot] = product


def kernel_2b(info, *refs):
    ins, early, along_y, along_x, acc = refs[:8], refs[8], refs[9:13], refs[13:15], refs[15]
    for slot, product in enumerate(products(PLAN_2B, ins, info)):
        acc[info[AT + NF + NF // 2 + slot]] = product
    for slot in range(NF // 2):
        acc[info[AT + NF + slot]] = early[slot]
    cut = along_y[0].shape[1]
    for s in range(NF):
        along_y[s // 2][s % 2] = acc[s, :cut]
        along_x[s % 2][s // 2] = acc[s, cut:]


def items_kernel(info, one_ref, one_ref_, up, up_, a, b, c, d, *outs):
    rows = one_ref.shape[1]
    one = one_ref[...] + one_ref_[:rows]
    lower = (a[...] + b[...]) + (c[...] + d[...])
    two = jnp.concatenate([up[...] + up_[...], lower], axis=0)
    choices = [x.astype(jnp.bfloat16) for x in (one, one.T, two, two.T)]
    for n, out in enumerate(outs):
        value = choices[3]
        for q in (2, 1, 0):
            value = jnp.where(info[SENDS + n] == q, choices[q], value)
        out[...] = value


def place_kernel(weight, info, *refs):
    got, pieces, (total, total_, first), (out, scores), diagonal = (
        refs[:4], refs[4:8], refs[8:11], refs[11:13], refs[13]
    )
    rows = out.shape[0]
    piece = 2 * rows // NF
    half = first.shape[1]
    for dy, source in enumerate(pieces):
        at = pl.multiple_of((info[Y] ^ dy) * piece, piece)
        diagonal[pl.ds(at, piece), :half] = source[rows : rows + piece].astype(jnp.bfloat16)
        diagonal[pl.ds(at, piece), half:] = source[rows + piece :].astype(jnp.bfloat16)
    values = [x[...] for x in got]
    for s in range(4):
        value = diagonal[...]
        for q in range(4):
            value = jnp.where(info[TAKES + s] == q, values[q], value)
        out[:, s * rows : (s + 1) * rows] = value
    scores[...] = first[...] - weight * (total[...] + total_[...])


def call(kernel, info, operands, outs, scratch=(), flops=0):
    vmem = pl.BlockSpec(memory_space=pltpu.VMEM)
    moved = sum(x.size * x.dtype.itemsize for x in (*operands, *outs))
    return pl.pallas_call(
        kernel,
        in_specs=[pl.BlockSpec(memory_space=pltpu.SMEM)] + [vmem] * len(operands),
        out_specs=[vmem] * len(outs),
        out_shape=list(outs),
        scratch_shapes=list(scratch),
        compiler_params=pltpu.CompilerParams(vmem_limit_bytes=24 * 2**20),
        cost_estimate=pl.CostEstimate(flops=flops, bytes_accessed=moved, transcendentals=0),
    )(info, *operands)


def array(dtype, *shape):
    return jax.ShapeDtypeStruct(shape, dtype)


def body(proj_grads, val_grads):
    rows, depth = proj_grads.shape
    pair_weight = 1.0 / rows**0.5
    tile_flops = 2 * rows * rows * depth
    table = reducers()
    perms, sends, takes = routes(table)
    me = lax.axis_index("dp") * NF + lax.axis_index("feat")
    info = jnp.asarray(facts(table, sends, takes))[me]
    f32, bf16 = jnp.float32, jnp.bfloat16

    def move(x, perm):
        return lax.ppermute(x, "dp", perm)

    def from_feat(x, s):
        return lax.ppermute(x, "feat", [(f, f ^ s) for f in range(NF)])

    def over_y(parts, n=None):
        parts = [parts[0]] + [from_feat(parts[dy], 2 * dy) for dy in (1, 2, 3)]
        a, b, c, d = [p[:n] for p in parts]
        return (a + b) + (c + d), parts

    own = proj_grads
    cut = rows // 2
    up1 = [move(own[:cut], FROM_ABOVE), move(own[cut:], FROM_ABOVE)]
    down1 = move(own, FROM_BELOW)
    side = move(own, OTHER_COLUMN)
    own_ = move(own, OTHER_CORE)

    first = jnp.dot(own, val_grads, preferred_element_type=f32)
    first, _ = over_y([first] * 4)
    first_ = from_feat(first, 1)

    high = 5 * rows // 8
    up2 = [move(up1[0], FROM_ABOVE), move(up1[1], FROM_ABOVE)]
    down2 = move(down1, FROM_BELOW)
    down1_ = move(down1, OTHER_CORE)

    one = call(
        kernel_1,
        info,
        (down1, down1_, own, own_, *up1, side),
        [array(f32, 2 * rows + 2 * rows // NF, rows)] * 4,
        [pltpu.VMEM((NF + 1, rows, rows), f32)],
        (NF + 1) * tile_flops,
    )
    parts = [one[0]] + [from_feat(one[dy], 2 * dy) for dy in (1, 2, 3)]
    one, send_ = (
        (a + b) + (c + d) for a, b, c, d in ([p[:rows] for p in parts], [p[rows:] for p in parts])
    )

    half = depth // 2
    q = first.shape[1]
    first, mine, other = call(
        hdot_kernel,
        info,
        (own, first, first_),
        [array(f32, rows, q), array(f32, half, q), array(f32, half, q)],
        flops=6 * rows * depth * q,
    )
    other = move(other, OTHER_CORE)
    mine = mine + other
    far = [move(up2[0], OTHER_COLUMN), move(up2[1], OTHER_COLUMN)]
    mine, far[0] = lax.optimization_barrier((mine, far[0]))
    chips = 2 * NZ
    mine = exchange(mine.reshape(chips, -1, mine.shape[1]), "dp", CHIP_GROUPS)
    mine = mine.sum(axis=0)
    mine = exchange(jnp.broadcast_to(mine, (chips, *mine.shape)), "dp", CHIP_GROUPS)
    mine = mine.reshape(half, -1)

    down2_ = move(down2, OTHER_CORE)
    (early,) = call(
        kernel_2a,
        info,
        (down2, down2_, *up1, side),
        [array(f32, NF // 2, rows, rows)],
        flops=4 * tile_flops,
    )
    two = call(
        kernel_2b,
        info,
        (down2, down2_, down1, down1_, *up2, *far, early),
        [array(f32, 2, high, rows)] * 4 + [array(f32, 4, rows - high, rows)] * 2,
        [pltpu.VMEM((NF, rows, rows), f32)],
        4 * tile_flops,
    )
    upper = [two[0]] + [from_feat(two[dy], 2 * dy) for dy in (1, 2, 3)]
    lower_ = from_feat(two[5], 1)
    one_ = from_feat(send_, 1)
    one_part = send_
    piece = 2 * rows // NF
    upper = (upper[0] + upper[1]) + (upper[2] + upper[3])
    lower = [two[4][dy] + lower_[dy] for dy in range(4)]
    upper, send_ = upper[0], upper[1]
    upper_ = from_feat(send_, 1)
    lower = [lower[0]] + [from_feat(lower[dy], 2 * dy) for dy in (1, 2, 3)]

    other = move(mine, OTHER_CORE)
    (shared,) = call(
        gdot_kernel,
        info,
        (own, mine, other, first, one_part, one_),
        [array(f32, rows + 2 * piece, q)],
        flops=6 * rows * depth * q,
    )
    total, pieces = over_y([shared] * 4, rows)
    total_ = from_feat(total, 1)

    out = call(items_kernel, info, (one, one_, upper, upper_, *lower), [array(bf16, rows, rows)] * 4)
    got = []
    for c in range(4):
        got.append(lax.ppermute(out[c], ("dp", "feat"), perms[c]))
    return tuple(
        call(
            functools.partial(place_kernel, pair_weight),
            info,
            (*got, *pieces, total, total_, first),
            [array(bf16, rows, 4 * rows), array(f32, rows, q)],
            [pltpu.VMEM((rows, rows), bf16)],
        )
    )


def solution(mesh):
    return jax.shard_map(
        body,
        mesh=mesh,
        in_specs=(P("dp", "feat"), P("feat", None)),
        out_specs=(P("dp", "feat"), P("dp", None)),
        check_vma=False,
    )
```

```python
import functools

import jax
import jax.numpy as jnp
import numpy as np
from jax import lax
from jax.experimental import pallas as pl
from jax.experimental.pallas import tpu as pltpu
from jax.sharding import PartitionSpec as P


NZ, NF = 8, 8


def row_block(a, z, k):
    return (a % 2) * 2 * NZ + (z % NZ) * 2 + (k % 2)


PLACES = [(a, z, k) for a in range(2) for z in range(NZ) for k in range(2)]


def shift(to):
    return [(row_block(*p), row_block(*to(*p))) for p in PLACES]


FROM_ABOVE = shift(lambda a, z, k: (a, z - 1, k))
FROM_BELOW = shift(lambda a, z, k: (a, z + 1, k))
OTHER_COLUMN = shift(lambda a, z, k: (1 - a, z, k))
OTHER_CORE = shift(lambda a, z, k: (a, z, 1 - k))


CHIP_GROUPS = [[row_block(a, z, k) for a in range(2) for z in range(NZ)] for k in range(2)]


def pair_lists(a, z, k):
    o, j = 1 - a, 1 - k
    sel = k if a == 0 else j
    low = k if z < NZ // 2 else j
    blk = row_block
    one = [
        (blk(a, z - 1, k), blk(a, z + 1, k)),
        (blk(a, z - 1, j), blk(a, z + 1, k)),
        (blk(a, z - 1, k), blk(o, z, k)),
        (blk(a, z - 1, j), blk(o, z, k)),
        (blk(a, z, k), blk(a, z + 1, k)),
        (blk(a, z, j), blk(a, z + 1, k)),
        (blk(a, z, j), blk(a, z, k)),
        (blk(a, z, sel), blk(o, z, k)),
    ]
    two = [
        (blk(a, z - 2, k), blk(a, z + 1, k)),
        (blk(a, z - 2, j), blk(a, z + 1, k)),
        (blk(a, z - 2, k), blk(o, z, k)),
        (blk(a, z - 2, j), blk(o, z, k)),
        (blk(a, z - 2, low), blk(a, z + 2, k)),
        (blk(a, z - 1, k), blk(o, z + 2, k)),
        (blk(a, z - 1, j), blk(o, z + 2, k)),
        (blk(a, z - 2, sel), blk(o, z + 2, k)),
    ]
    return one, two


def colour_edges(edges, n_colours):
    at_src, at_dst = {}, {}
    colour = [None] * len(edges)

    def free(table, node):
        return next(c for c in range(n_colours) if (node, c) not in table)

    for e, (s, d) in enumerate(edges):
        c1, c2 = free(at_src, s), free(at_dst, d)
        if c1 != c2:
            path, node, side, c = [], d, 1, c1
            while True:
                nxt = (at_dst if side else at_src).get((node, c))
                if nxt is None:
                    break
                path.append(nxt)
                node = edges[nxt][0 if side else 1]
                side, c = 1 - side, c1 + c2 - c
            for q in path:
                at_src.pop((edges[q][0], colour[q]))
                at_dst.pop((edges[q][1], colour[q]))
            for q in path:
                colour[q] = c1 + c2 - colour[q]
                at_src[(edges[q][0], colour[q])] = q
                at_dst[(edges[q][1], colour[q])] = q
        colour[e] = c1
        at_src[(s, c1)] = e
        at_dst[(d, c1)] = e
    return colour


SIZES = (2 * 2, NF // 2, NZ)


def chip(i, f):
    return f % 2 * 2 + i // (2 * NZ), f // 2, i // 2 % NZ


def hops(src, dst):
    return sum(min((x - y) % n, (y - x) % n) for x, y, n in zip(src, dst, SIZES))


def links(src, dst, memo):
    if (src, dst) not in memo:
        at, part = [], []
        for k, axes in enumerate(((2, 1, 0), (2, 0, 1))):
            here = list(src)
            for axis in axes:
                n = SIZES[axis]
                ahead = (dst[axis] - here[axis]) % n
                ways = [(1, ahead), (-1, n - ahead)]
                short = [w for w in ways if w[1] == min(ahead, n - ahead)]
                for sign, steps in short:
                    now = list(here)
                    for _ in range(steps):
                        at.append(np.ravel_multi_index((k, axis, (1 + sign) // 2, *now), (2, 3, 2, *SIZES)))
                        part.append(1.0 / len(short))
                        now[axis] = (now[axis] + sign) % n
                here[axis] = dst[axis]
        memo[src, dst] = np.array(at, np.int64), np.array(part)
    return memo[src, dst]


def reducers():
    per = len(PLACES) // NF
    table = np.tile(np.arange(NF, dtype=np.int32), (len(PLACES), 2, 1))
    memo, load, owners, far = {}, np.zeros(2 * 3 * 2 * len(PLACES) * NF // 2), {}, {}
    for p in PLACES:
        i = row_block(*p)
        for round_, pairs in enumerate(pair_lists(*p)):
            for slot, (r, c) in enumerate(pairs):
                ends = [chip(r, c // per), chip(c, r // per)][: 1 if (round_, slot) == (0, 6) else 2]
                owners[i, round_, slot] = ends
                for f in range(NF):
                    far[i, round_, slot, f] = 30 * sum(hops(chip(i, f), dst) ** 3 for dst in ends)

    def put(key, f, weight):
        for dst in owners[key]:
            at, part = links(chip(key[0], f), dst, memo)
            np.add.at(load, at, weight * part)

    def swap(a, b, f, g):
        for key, old, new in ((a, f, g), (b, g, f)):
            put(key, old, -1)
            put(key, new, 1)

    for key in owners:
        put(key, int(table[key]), 1)
    for sweep in range(10):
        power = 4 if sweep >= 3 else 0
        for i in range(len(PLACES)):
            for round_ in range(2):
                for p in range(NF):
                    for q in range(p):
                        a, b = (i, round_, p), (i, round_, q)
                        f, g = int(table[a]), int(table[b])
                        before = (load**power).sum() + far[(*a, f)] + far[(*b, g)]
                        swap(a, b, f, g)
                        if (load**power).sum() + far[(*a, g)] + far[(*b, f)] < before - 1e-6:
                            table[a], table[b] = g, f
                        else:
                            swap(a, b, g, f)
    return table


def routes(table):
    per = len(PLACES) // NF
    edges, what = [], []
    for p in PLACES:
        for round_, pairs in enumerate(pair_lists(*p)):
            for slot, (r, c) in enumerate(pairs):
                src = row_block(*p) * NF + int(table[row_block(*p), round_, slot])
                edges.append((src, r * NF + c // per))
                what.append((2 * round_, c % per))
                if not (round_ == 0 and slot == 6):
                    edges.append((src, c * NF + r // per))
                    what.append((2 * round_ + 1, r % per))
    by_hops = sorted(range(len(edges)), key=lambda e: -hops(*(chip(*divmod(x, NF)) for x in edges[e])))
    edges, what = [edges[e] for e in by_hops], [what[e] for e in by_hops]
    colour = colour_edges(edges, 4)
    n = len(PLACES) * NF
    perms = [[] for _ in range(4)]
    sends = np.zeros((n, 4), np.int32)
    takes = np.full((n, 4), -1, np.int32)
    for (s, d), (item, at), c in zip(edges, what, colour):
        perms[c].append((s, d))
        sends[s, c] = item
        assert takes[d, at] < 0
        takes[d, at] = c
    for i in range(len(PLACES)):
        assert takes[i * NF + i // per, i % per] < 0
        takes[i * NF + i // per, i % per] = 4
    assert (takes >= 0).all()
    return perms, sends, takes


COLUMN_0, LOW_HALF, CORE, Y, AT, SENDS, TAKES = 0, 1, 2, 3, 4, 4 + 2 * NF, 8 + 2 * NF


def facts(table, sends, takes):
    rows = np.zeros((len(PLACES) * NF, 12 + 2 * NF), np.int32)
    for a, z, k in PLACES:
        i = row_block(a, z, k)
        for f in range(NF):
            at = table[i] ^ f
            rows[i * NF + f] = [
                a == 0, z < NZ // 2, k, f // 2, *at[0], *at[1], *sends[i * NF + f], *takes[i * NF + f]
            ]
    return rows


def exchange(value, axis, groups=None):
    return lax.all_to_all(
        value, axis, split_axis=0, concat_axis=0, tiled=True, axis_index_groups=groups
    )


def parts_of(x):
    high = x.astype(jnp.bfloat16)
    rest = x - high.astype(jnp.float32)
    mid = rest.astype(jnp.bfloat16)
    low = (rest - mid.astype(jnp.float32)).astype(jnp.bfloat16)
    return jnp.concatenate([high, mid, low], axis=-1)


def three(y):
    q = y.shape[-1] // 3
    return (y[:, 2 * q :] + y[:, q : 2 * q]) + y[:, :q]


def hdot_kernel(info, own, part, part_, first, mine, other):
    value = part[...] + part_[...]
    first[...] = value
    terms = parts_of(value)
    half = mine.shape[0]
    for at in range(2):
        rows = three(
            lax.dot_general(
                own[:, at * half : (at + 1) * half],
                terms,
                (((0,), (0,)), ((), ())),
                preferred_element_type=jnp.float32,
            )
        )

        @pl.when(info[CORE] == at)
        def _():
            mine[...] = rows

        @pl.when(info[CORE] != at)
        def _():
            other[...] = rows


def share_kernel(info, parts, out):
    total = parts[0]
    for i in range(1, parts.shape[0]):
        total = total + parts[i]
    for i in range(parts.shape[0]):
        out[i] = total


def gdot_kernel(info, own, mine, other, first, one, one_, out):
    half = mine.shape[0]
    total = None
    for at in range(2):
        back = jnp.where(info[CORE] == at, mine[...], other[...])
        term = three(
            jnp.dot(
                own[:, at * half : (at + 1) * half], parts_of(back), preferred_element_type=jnp.float32
            )
        )
        total = term if total is None else total + term
    wide = own[...].astype(jnp.float32)
    rows, q = first.shape
    out[:rows] = total - jnp.sum(wide * wide, axis=1, keepdims=True) * first[...]
    square = one[rows:] + one_[rows:]
    piece = square.shape[0]
    out[rows : rows + piece] = square[:, :q]
    out[rows + piece :] = square[:, q:]


def tile(left, right):
    return lax.dot_general(
        left, right, (((1,), (1,)), ((), ())), preferred_element_type=jnp.float32
    )


def products(plan, ins, info):
    for left, right in plan:
        if isinstance(left, tuple):
            i, j, flag = left
            value = jnp.where(info[flag] > 0, ins[i][...], ins[j][...])
        else:
            value = ins[left][...]
        if isinstance(right, tuple):
            against = jnp.concatenate([ins[i][...] for i in right], axis=0)
        else:
            against = ins[right][...]
        yield tile(value, against)


UP = (4, 5)
PLAN_1 = ((0, UP), (1, UP), (2, UP), (3, UP), (0, 6), (1, 6), ((2, 3, COLUMN_0), 6), (3, 2))
SLOTS_1 = (0, 1, 4, 5, 2, 3, 7, 6)
PLAN_2A = ((0, (2, 3)), (1, (2, 3)), (0, 4), (1, 4))
PLAN_2B = (((0, 1, LOW_HALF), (4, 5)), (2, (6, 7)), (3, (6, 7)), ((0, 1, COLUMN_0), (6, 7)))


def kernel_1(info, *refs):
    ins, outs, acc = refs[:7], refs[7:11], refs[11]
    for slot, product in zip(SLOTS_1, products(PLAN_1, ins, info)):
        acc[info[AT + slot]] = product
    square = tile(ins[2][...], ins[2][...])
    rows = square.shape[0]
    own = lax.broadcasted_iota(jnp.int32, (rows, rows), 0)
    other = lax.broadcasted_iota(jnp.int32, (rows, rows), 1)
    acc[NF] = jnp.where(own == other, 0.0, square)
    piece = 2 * rows // NF
    for dy, out in enumerate(outs):
        out[:rows] = acc[2 * dy]
        out[rows : 2 * rows] = acc[2 * dy + 1]
        at = pl.multiple_of((info[Y] ^ dy) * piece, piece)
        out[2 * rows :] = acc[NF, pl.ds(at, piece)]


def kernel_2a(info, *refs):
    for slot, product in enumerate(products(PLAN_2A, refs[:5], info)):
        refs[5][slot] = product


def kernel_2b(info, *refs):
    ins, early, along_y, along_x, acc = refs[:8], refs[8], refs[9:13], refs[13:15], refs[15]
    for slot, product in enumerate(products(PLAN_2B, ins, info)):
        acc[info[AT + NF + NF // 2 + slot]] = product
    for slot in range(NF // 2):
        acc[info[AT + NF + slot]] = early[slot]
    cut = along_y[0].shape[1]
    for s in range(NF):
        along_y[s // 2][s % 2] = acc[s, :cut]
        along_x[s % 2][s // 2] = acc[s, cut:]


def items_kernel(info, one_ref, one_ref_, up, up_, a, b, c, d, *outs):
    rows = one_ref.shape[1]
    one = one_ref[...] + one_ref_[:rows]
    lower = (a[...] + b[...]) + (c[...] + d[...])
    two = jnp.concatenate([up[...] + up_[...], lower], axis=0)
    choices = [x.astype(jnp.bfloat16) for x in (one, one.T, two, two.T)]
    for n, out in enumerate(outs):
        value = choices[3]
        for q in (2, 1, 0):
            value = jnp.where(info[SENDS + n] == q, choices[q], value)
        out[...] = value


def place_kernel(weight, info, *refs):
    got, pieces, (total, total_, first), (out, scores), diagonal = (
        refs[:4], refs[4:8], refs[8:11], refs[11:13], refs[13]
    )
    rows = out.shape[0]
    piece = 2 * rows // NF
    half = first.shape[1]
    for dy, source in enumerate(pieces):
        at = pl.multiple_of((info[Y] ^ dy) * piece, piece)
        diagonal[pl.ds(at, piece), :half] = source[rows : rows + piece].astype(jnp.bfloat16)
        diagonal[pl.ds(at, piece), half:] = source[rows + piece :].astype(jnp.bfloat16)
    values = [x[...] for x in got]
    for s in range(4):
        value = diagonal[...]
        for q in range(4):
            value = jnp.where(info[TAKES + s] == q, values[q], value)
        out[:, s * rows : (s + 1) * rows] = value
    scores[...] = first[...] - weight * (total[...] + total_[...])


def call(kernel, info, operands, outs, scratch=(), flops=0):
    vmem = pl.BlockSpec(memory_space=pltpu.VMEM)
    moved = sum(x.size * x.dtype.itemsize for x in (*operands, *outs))
    return pl.pallas_call(
        kernel,
        in_specs=[pl.BlockSpec(memory_space=pltpu.SMEM)] + [vmem] * len(operands),
        out_specs=[vmem] * len(outs),
        out_shape=list(outs),
        scratch_shapes=list(scratch),
        compiler_params=pltpu.CompilerParams(vmem_limit_bytes=24 * 2**20),
        cost_estimate=pl.CostEstimate(flops=flops, bytes_accessed=moved, transcendentals=0),
    )(info, *operands)


def array(dtype, *shape):
    return jax.ShapeDtypeStruct(shape, dtype)


def body(proj_grads, val_grads):
    rows, depth = proj_grads.shape
    pair_weight = 1.0 / rows**0.5
    tile_flops = 2 * rows * rows * depth
    table = reducers()
    perms, sends, takes = routes(table)
    me = lax.axis_index("dp") * NF + lax.axis_index("feat")
    info = jnp.asarray(facts(table, sends, takes))[me]
    f32, bf16 = jnp.float32, jnp.bfloat16

    def move(x, perm):
        return lax.ppermute(x, "dp", perm)

    def from_feat(x, s):
        return lax.ppermute(x, "feat", [(f, f ^ s) for f in range(NF)])

    def over_y(parts, n=None):
        parts = [parts[0]] + [from_feat(parts[dy], 2 * dy) for dy in (1, 2, 3)]
        a, b, c, d = [p[:n] for p in parts]
        return (a + b) + (c + d), parts

    own = proj_grads
    cut = rows // 2
    up1 = [move(own[:cut], FROM_ABOVE), move(own[cut:], FROM_ABOVE)]
    down1 = move(own, FROM_BELOW)
    side = move(own, OTHER_COLUMN)
    own_ = move(own, OTHER_CORE)

    first = jnp.dot(own, val_grads, preferred_element_type=f32)
    first, _ = over_y([first] * 4)
    first_ = from_feat(first, 1)

    high = 5 * rows // 8
    up2 = [move(up1[0], FROM_ABOVE), move(up1[1], FROM_ABOVE)]
    down2 = move(down1, FROM_BELOW)
    down1_ = move(down1, OTHER_CORE)

    one = call(
        kernel_1,
        info,
        (down1, down1_, own, own_, *up1, side),
        [array(f32, 2 * rows + 2 * rows // NF, rows)] * 4,
        [pltpu.VMEM((NF + 1, rows, rows), f32)],
        (NF + 1) * tile_flops,
    )
    parts = [one[0]] + [from_feat(one[dy], 2 * dy) for dy in (1, 2, 3)]
    one, send_ = (
        (a + b) + (c + d) for a, b, c, d in ([p[:rows] for p in parts], [p[rows:] for p in parts])
    )

    half = depth // 2
    q = first.shape[1]
    first, mine, other = call(
        hdot_kernel,
        info,
        (own, first, first_),
        [array(f32, rows, q), array(f32, half, q), array(f32, half, q)],
        flops=6 * rows * depth * q,
    )
    other = move(other, OTHER_CORE)
    mine = mine + other
    far = [move(up2[0], OTHER_COLUMN), move(up2[1], OTHER_COLUMN)]
    mine, far[0] = lax.optimization_barrier((mine, far[0]))
    chips = 2 * NZ
    mine = exchange(mine.reshape(chips, -1, mine.shape[1]), "dp", CHIP_GROUPS)
    (mine,) = call(share_kernel, info, (mine,), [array(f32, *mine.shape)])
    mine = exchange(mine, "dp", CHIP_GROUPS)
    mine = mine.reshape(half, -1)

    down2_ = move(down2, OTHER_CORE)
    (early,) = call(
        kernel_2a,
        info,
        (down2, down2_, *up1, side),
        [array(f32, NF // 2, rows, rows)],
        flops=4 * tile_flops,
    )
    two = call(
        kernel_2b,
        info,
        (down2, down2_, down1, down1_, *up2, *far, early),
        [array(f32, 2, high, rows)] * 4 + [array(f32, 4, rows - high, rows)] * 2,
        [pltpu.VMEM((NF, rows, rows), f32)],
        4 * tile_flops,
    )
    upper = [two[0]] + [from_feat(two[dy], 2 * dy) for dy in (1, 2, 3)]
    lower_ = from_feat(two[5], 1)
    one_ = from_feat(send_, 1)
    one_part = send_
    piece = 2 * rows // NF
    upper = (upper[0] + upper[1]) + (upper[2] + upper[3])
    lower = [two[4][dy] + lower_[dy] for dy in range(4)]
    upper, send_ = upper[0], upper[1]
    upper_ = from_feat(send_, 1)
    lower = [lower[0]] + [from_feat(lower[dy], 2 * dy) for dy in (1, 2, 3)]

    other = move(mine, OTHER_CORE)
    (shared,) = call(
        gdot_kernel,
        info,
        (own, mine, other, first, one_part, one_),
        [array(f32, rows + 2 * piece, q)],
        flops=6 * rows * depth * q,
    )
    total, pieces = over_y([shared] * 4, rows)
    total_ = from_feat(total, 1)

    out = call(items_kernel, info, (one, one_, upper, upper_, *lower), [array(bf16, rows, rows)] * 4)
    got = []
    for c in range(4):
        got.append(lax.ppermute(out[c], ("dp", "feat"), perms[c]))
    return tuple(
        call(
            functools.partial(place_kernel, pair_weight),
            info,
            (*got, *pieces, total, total_, first),
            [array(bf16, rows, 4 * rows), array(f32, rows, q)],
            [pltpu.VMEM((rows, rows), bf16)],
        )
    )


def solution(mesh):
    return jax.shard_map(
        body,
        mesh=mesh,
        in_specs=(P("dp", "feat"), P("feat", None)),
        out_specs=(P("dp", "feat"), P("dp", None)),
        check_vma=False,
    )
```
